32 devices in a mesh: kv: 4 (over z), seq: 8 (over y, x, core).
Axes of the slice: x: 2, y: 2, z: 4, core: 2. Of those that a mesh axis runs over, the one named last changes fastest.
Arguments:
- queries: bfloat16 [32, 64, 128], P('seq', 'kv'), may hold values from -1024 to 1024
- prompt_keys: bfloat16 [4, 32768, 128], P('kv', 'seq'), may hold values from -5 to 5
- prompt_values: bfloat16 [4, 32768, 128], P('kv', 'seq'), may hold values from -6 to 6
- branch_keys: bfloat16 [4, 8192, 128], P('kv', 'seq'), may hold values from -7 to 7
- branch_values: bfloat16 [4, 8192, 128], P('kv', 'seq'), may hold values from -6 to 6
- pool_keys: bfloat16 [256, 512, 4, 128], P(('kv', 'seq')), may hold values from -8 to 8
- pool_values: bfloat16 [256, 512, 4, 128], P(('kv', 'seq')), may hold values from -6 to 6
- suffix_lengths: int32 [32], replicated, may hold values from 1 to 6144, 49152 in all
- leaf_branch: int32 [32], replicated, may hold values from 0 to 1
- slot_item: int32 [256], replicated, may hold values from 0 to 255, as said below
Outputs:
- attention: bfloat16 [32, 64, 128], P('seq', 'kv')
The draws below stay inside these ranges and needn't reach their ends.
Inputs may be any that keep to these rules, and one draw needn't show every extreme that they name: `suffix_lengths`: the lengths sum to 49152 and the largest is exactly 6144. `slot_item`: A permutation of the page numbers; pages whose entry is at least the total count of suffix blocks hold no live tokens.
All inputs are finite; a program needn't handle non-finite values.
Results may differ from the reference program's by a relative error of at most 0.0065.
Values may be sent and summed in bfloat16 or wider, within the bound.
A program may use at most 128 MiB of HBM per device.

```python
import math
import jax
import jax.numpy as jnp
import numpy as np
from jax import lax

HD = 128
G = 16
KVH = 4
HEADS = 64
P_DEV = 4096
P_SIZE = 32768
BR_LEN = 4096
BRANCHES = 2
LEAVES = 32
BLOCK = 512
SUF_MEAN = 1536
SUF_MOST = 6144
SLOTS = 8
POOL = 256
N_SEQ = 8


def prompt_rows(key):
    base_rows = jax.random.truncated_normal(jax.random.fold_in(key, 101), -5.0, 5.0, (KVH, P_SIZE, HD), jnp.float32)
    return base_rows


def draw_prompt_keys(key, part):
    return prompt_rows(key).astype(jnp.bfloat16)


def draw_queries(key, part):
    full_shape = (LEAVES, HEADS, HD)
    values_all = 2.5 * jax.random.truncated_normal(jax.random.fold_in(key, 202), -6.0, 6.0, full_shape, jnp.float32)
    return values_all.astype(jnp.bfloat16)


def draw_slot_item(key, part):
    first_key, second_key = jax.random.split(jax.random.fold_in(key, 303))
    devices_all = POOL // SLOTS
    levels = jax.random.randint(first_key, (devices_all,), 0, 4)
    jitter = jax.random.randint(second_key, (POOL,), 0, 64)
    ranking = (jnp.repeat(levels, SLOTS) * 64 + jitter) * POOL + jnp.arange(POOL, dtype=jnp.int32)
    ordering = jnp.argsort(ranking, stable=True)
    return jnp.zeros((POOL,), jnp.int32).at[ordering].set(jnp.arange(POOL, dtype=jnp.int32))


def with_ends(entries, key, smallest, largest):
    place = [jax.random.randint(jax.random.fold_in(key, axis), (), 0, length) for axis, length in enumerate(entries.shape)]
    main_axis = entries.shape.index(max(entries.shape))
    neighbour = place[:main_axis] + [(place[main_axis] + 1) % entries.shape[main_axis]] + place[main_axis + 1:]
    return entries.at[tuple(place)].set(smallest).at[tuple(neighbour)].set(largest)


def steps_of(rng, extent, cuts, least, high):
    level, own = 1.0, jax.random.fold_in(rng, 6)
    for dim, shards_of in cuts:
        heights = jnp.exp(jax.random.uniform(jax.random.fold_in(own, dim), (shards_of,), jnp.float32, least / len(cuts), high / len(cuts)))
        level = level * jnp.repeat(heights, extent[dim] // shards_of).reshape([-1 if axis == dim else 1 for axis in range(len(extent))])
    return level


def split_up(number_of, total, bound, slope):
    portions = [(1 << 20) // math.isqrt(grade ** slope) + 1 for grade in range(2, number_of + 1)]
    rest, given = total - bound - (number_of - 1), [1] * (number_of - 1)
    while rest > 0:
        candidates = [i for i in range(number_of - 1) if given[i] < bound]
        pool, left = sum([portions[i] for i in candidates]), rest
        for i in candidates:
            extra = min(bound - given[i], max(1, left * portions[i] // pool), rest)
            given[i] = given[i] + extra
            rest = rest - extra
    return np.array([bound] + given)


def ragged(stream_key, amount, total, most, slope):
    if amount == 2:
        one = jax.random.randint(stream_key, (), max(1, total - most), min(most, total - 1) + 1)
        return jnp.stack([one, total - one])
    sizes = jnp.asarray(split_up(amount, total, most, slope), jnp.int32)
    twos = (amount - 1) // 2
    giver, receiver = sizes[1:1 + 2 * twos:2], sizes[2:2 + 2 * twos:2]
    margin = jnp.minimum(giver - 1, most - receiver)
    moved = jax.random.randint(jax.random.fold_in(stream_key, 1), (twos,), 0, 1 << 20) % (margin + 1)
    sizes = sizes.at[1:1 + 2 * twos:2].set(giver - moved).at[2:2 + 2 * twos:2].set(receiver + moved)
    return sizes[jax.random.permutation(jax.random.fold_in(stream_key, 2), amount)]


def noise(rng, extent, deviation, bound, pieces=(), held_as=jnp.bfloat16):
    loudness = steps_of(rng, extent, pieces, -0.22, 0.18) if pieces else 1.0
    array = jax.random.normal(rng, extent, jnp.float32) * deviation * loudness
    return jnp.minimum(jnp.maximum(array, -bound), bound).astype(held_as)


def setup_inputs(seed: int = 0) -> dict:
    splits = jax.random.split(jax.random.key(seed), 11)
    return {
        "queries": draw_queries(jax.random.fold_in(splits[10], 71), 0),
        "prompt_keys": draw_prompt_keys(jax.random.fold_in(splits[10], 71), 0),
        "prompt_values": noise(splits[2], (KVH, P_SIZE, HD), 1.0, 6.0, ((0, 4), (1, 8))),
        "branch_keys": noise(splits[3], (KVH, BRANCHES * BR_LEN, HD), 1.15, 7.0, ((0, 4), (1, 8))),
        "branch_values": noise(splits[4], (KVH, BRANCHES * BR_LEN, HD), 1.0, 6.0, ((0, 4), (1, 8))),
        "pool_keys": noise(splits[5], (POOL, BLOCK, KVH, HD), 1.3, 8.0, ((0, 32),)),
        "pool_values": noise(splits[6], (POOL, BLOCK, KVH, HD), 1.0, 6.0, ((0, 32),)),
        "suffix_lengths": ragged(splits[7], LEAVES, LEAVES * SUF_MEAN, SUF_MOST, 2).astype(jnp.int32),
        "leaf_branch": with_ends(jax.random.randint(splits[8], (LEAVES,), 0, BRANCHES), jax.random.fold_in(splits[8], 1), 0, BRANCHES - 1).astype(jnp.int32),
        "slot_item": draw_slot_item(jax.random.fold_in(splits[10], 71), 0),
    }


NEG_FILL = -1e+30

def page_layout(suffix_lengths, slot_item):
    block_count = ((suffix_lengths + BLOCK - 1) // BLOCK).astype(jnp.int32)
    block_ends = jnp.cumsum(block_count).astype(jnp.int32)
    block_starts = (block_ends - block_count).astype(jnp.int32)
    owner = (slot_item[:, None] >= block_starts[None, :]) & (slot_item[:, None] < block_ends[None, :])
    inner = slot_item - lax.optimization_barrier(jnp.sum(jnp.where(owner, block_starts[None, :], 0), axis=1)).astype(jnp.int32)
    length_of = lax.optimization_barrier(jnp.sum(jnp.where(owner, suffix_lengths[None, :], 0), axis=1)).astype(jnp.int32)
    valid = jnp.clip(length_of - inner * BLOCK, 0, BLOCK).astype(jnp.int32)
    return (owner, valid)

def rounded(values):
    return lax.optimization_barrier(values.astype(jnp.bfloat16)).astype(jnp.float32)

def reference(queries, prompt_keys, prompt_values, branch_keys, branch_values, pool_keys, pool_values, suffix_lengths, leaf_branch, slot_item):
    inv_root = 1.0 / math.sqrt(HD)
    highest = lax.Precision.HIGHEST
    owner, valid = page_layout(suffix_lengths, slot_item)
    owner_f = owner.astype(jnp.float32)
    leaf_ids = lax.optimization_barrier(jnp.sum(jnp.where(owner, jnp.arange(LEAVES, dtype=jnp.int32)[None, :], 0), axis=1)).astype(jnp.int32)
    page_mask = jnp.arange(BLOCK, dtype=jnp.int32)[None, :] < valid[:, None]

    def one_head(packed):
        head_index, keys_p, values_p, keys_b, values_b = packed
        query_f = lax.dynamic_slice_in_dim(queries, head_index * G, G, 1).astype(jnp.float32)
        query_rows = query_f.reshape(LEAVES * G, HD)
        prompt_k = keys_p.reshape(N_SEQ, P_DEV, HD)
        prompt_v = values_p.reshape(N_SEQ, P_DEV, HD)

        def prompt_max(carry, key_block):
            scores = jnp.dot(query_rows, key_block.astype(jnp.float32).T, precision=highest) * inv_root
            return (jnp.maximum(carry, lax.optimization_barrier(jnp.max(scores, axis=1))), None)
        top_prompt = lax.scan(prompt_max, jnp.full((LEAVES * G,), NEG_FILL, jnp.float32), prompt_k)[0]
        branch_k = keys_b.reshape(BRANCHES, BR_LEN, HD)[leaf_branch].astype(jnp.float32)
        branch_v = values_b.reshape(BRANCHES, BR_LEN, HD)[leaf_branch].astype(jnp.float32)
        scores_b = jnp.einsum('lgd,lnd->lgn', query_f, branch_k, precision=highest) * inv_root
        pool_k = lax.dynamic_index_in_dim(pool_keys, head_index, 2, keepdims=False).astype(jnp.float32)
        pool_v = lax.dynamic_index_in_dim(pool_values, head_index, 2, keepdims=False).astype(jnp.float32)
        page_q = query_f[leaf_ids]
        scores_s = jnp.einsum('pgd,pbd->pgb', page_q, pool_k, precision=highest) * inv_root
        scores_s = jnp.where(page_mask[:, None, :], scores_s, NEG_FILL)
        page_top = lax.optimization_barrier(jnp.max(scores_s, axis=2))
        suffix_top = lax.optimization_barrier(jnp.max(jnp.where(owner[:, :, None], page_top[:, None, :], NEG_FILL), axis=0))
        top = jnp.maximum(jnp.maximum(top_prompt.reshape(LEAVES, G), lax.optimization_barrier(jnp.max(scores_b, axis=2))), suffix_top)
        top_rows = top.reshape(LEAVES * G)

        def prompt_sum(carry, pair):
            key_block, value_block = pair
            scores = jnp.dot(query_rows, key_block.astype(jnp.float32).T, precision=highest) * inv_root
            expo = jnp.exp(scores - top_rows[:, None])
            numer_part = jnp.dot(rounded(expo), value_block.astype(jnp.float32), precision=highest)
            return ((carry[0] + lax.optimization_barrier(jnp.sum(expo, axis=1)), carry[1] + numer_part), None)
        start = (jnp.zeros((LEAVES * G,), jnp.float32), jnp.zeros((LEAVES * G, HD), jnp.float32))
        denom, numer = lax.scan(prompt_sum, start, (prompt_k, prompt_v))[0]
        expo_b = jnp.exp(scores_b - top[:, :, None])
        denom = denom + lax.optimization_barrier(jnp.sum(expo_b, axis=2)).reshape(LEAVES * G)
        numer = numer + jnp.einsum('lgn,lnd->lgd', rounded(expo_b), branch_v, precision=highest).reshape(LEAVES * G, HD)
        page_ref = top[leaf_ids]
        expo_s = jnp.where(page_mask[:, None, :], jnp.exp(scores_s - page_ref[:, :, None]), 0.0)
        page_num = jnp.einsum('pgb,pbd->pgd', rounded(expo_s), pool_v, precision=highest)
        denom = denom + jnp.einsum('pl,pg->lg', owner_f, lax.optimization_barrier(jnp.sum(expo_s, axis=2)), precision=highest).reshape(LEAVES * G)
        numer = numer + jnp.einsum('pl,pgd->lgd', owner_f, page_num, precision=highest).reshape(LEAVES * G, HD)
        return (numer / denom[:, None]).astype(jnp.bfloat16).reshape(LEAVES, G, HD)
    heads_out = lax.map(one_head, (jnp.arange(KVH, dtype=jnp.int32), prompt_keys, prompt_values, branch_keys, branch_values))
    return jnp.transpose(heads_out, (1, 0, 2, 3)).reshape(LEAVES, HEADS, HD)
```

```python
import functools
import math

import jax
import jax.numpy as jnp
from jax import lax
from jax.experimental import pallas as pl
from jax.experimental.pallas import tpu as pltpu
from jax.sharding import PartitionSpec as P

G = 16
BR_LEN = 4096
NEG = -1e30
LANES = 128
CHUNK = 1024
MESH = pl.DeviceIdType.MESH
NT = (((1,), (1,)), ((), ()))


def kernel(
    kv_count,
    seq_count,
    lengths,
    branch_of,
    items,
    queries,
    prompt_k,
    prompt_v,
    branch_k,
    branch_v,
    pool_k,
    pool_v,
    out,
    ends,
    leaf_of,
    valid_of,
    kbuf,
    vbuf,
    pkbuf,
    pvbuf,
    q_all,
    q_send,
    q_page,
    row_branch,
    head_bias,
    s_buf,
    row_top,
    row_sum,
    row_num,
    stat_top,
    stat_sum,
    num_send,
    num_recv,
    stat_send,
    stat_recv,
    fin_num_send,
    fin_num_recv,
    fin_stat_send,
    fin_stat_recv,
    load_sem,
    page_sem,
    own_sem,
    q_ssem,
    q_rsem,
    p_ssem,
    p_rsem,
    n_ssem,
    n_rsem,
    f_ssem,
    f_rsem,
):
    kv_me = lax.axis_index("kv")
    seq_me = lax.axis_index("seq")
    leaf_dev = queries.shape[0]
    head_dim = queries.shape[2]
    leaves = leaf_dev * seq_count
    rows = leaves * G
    own_rows = leaf_dev * G
    slots, page_rows = pool_k.shape[0], pool_k.shape[1]
    block = page_rows // kv_count
    prompt_rows, branch_rows = prompt_k.shape[0], branch_k.shape[0]
    keys = prompt_rows + branch_rows
    col_w = num_send.shape[1]
    n_col = kv_count * col_w
    heads_all = kv_count * G
    scale = math.log2(math.e) / math.sqrt(head_dim)
    row_block = min(256, rows // 2)

    loads = [
        pltpu.make_async_copy(prompt_k, kbuf.at[pl.ds(0, prompt_rows)], load_sem.at[0]),
        pltpu.make_async_copy(branch_k, kbuf.at[pl.ds(prompt_rows, branch_rows)], load_sem.at[1]),
        pltpu.make_async_copy(prompt_v, vbuf.at[pl.ds(0, prompt_rows)], load_sem.at[2]),
        pltpu.make_async_copy(branch_v, vbuf.at[pl.ds(prompt_rows, branch_rows)], load_sem.at[3]),
    ]
    page_loads = []
    for s in range(slots):
        page_loads.append(pltpu.make_async_copy(pool_k.at[s], pkbuf.at[s], page_sem.at[0, s]))
        page_loads.append(pltpu.make_async_copy(pool_v.at[s], pvbuf.at[s], page_sem.at[1, s]))
    own_q = pltpu.make_async_copy(
        queries, q_all.at[pl.ds(seq_me * leaf_dev, leaf_dev)], own_sem.at[0]
    )

    seq_peers = [lax.rem(seq_me + o, seq_count) for o in range(seq_count)]
    kv_peers = [lax.rem(kv_me + o, kv_count) for o in range(kv_count)]

    barrier = pltpu.get_barrier_semaphore()
    for o in range(1, kv_count):
        pl.semaphore_signal(barrier, inc=1, device_id=(kv_peers[o], seq_me), device_id_type=MESH)
    for o in range(1, seq_count):
        pl.semaphore_signal(barrier, inc=1, device_id=(kv_me, seq_peers[o]), device_id_type=MESH)
    own_q.start()
    for copy in loads:
        copy.start()
    for copy in page_loads:
        copy.start()

    total = jnp.int32(0)
    for l in range(leaves):
        total = total + (lengths[l] + (block - 1)) // block
        ends[l] = total
    for j in range(kv_count):
        for s in range(slots):
            item = items[(j * seq_count + seq_me) * slots + s]

            def count(l, acc, item=item):
                return acc + (item >= ends[l]).astype(jnp.int32)

            leaf_of[j * slots + s] = lax.fori_loop(0, leaves, count, jnp.int32(0), unroll=True)
    for s in range(slots):
        item = items[(kv_me * seq_count + seq_me) * slots + s]
        leaf = leaf_of[kv_me * slots + s]
        safe = jnp.minimum(leaf, leaves - 1)
        length = lengths[safe]
        start = ends[safe] - (length + (block - 1)) // block
        live = jnp.clip(length - (item - start) * block, 0, block)
        valid_of[s] = jnp.where(leaf < leaves, live, 0)

    for l in range(leaves):
        row_branch[pl.ds(l * G, G), :] = jnp.full((G, LANES), branch_of[l], jnp.int32)
    bias_col = lax.broadcasted_iota(jnp.int32, (heads_all, page_rows), 1) % kv_count
    bias_row = lax.broadcasted_iota(jnp.int32, (heads_all, page_rows), 0) // G
    head_bias[...] = jnp.where(bias_col == bias_row, 0.0, NEG)
    stat_top[...] = jnp.zeros_like(stat_top)
    stat_sum[...] = jnp.zeros_like(stat_sum)
    stat_send[...] = jnp.zeros_like(stat_send)
    fin_stat_send[...] = jnp.zeros_like(fin_stat_send)
    if col_w > slots * G:
        num_send[...] = jnp.zeros_like(num_send)

    pl.semaphore_wait(barrier, kv_count + seq_count - 2)

    q_copies = []
    for o in range(seq_count - 1, 0, -1):
        copy = pltpu.make_async_remote_copy(
            src_ref=queries,
            dst_ref=q_all.at[pl.ds(seq_me * leaf_dev, leaf_dev)],
            send_sem=q_ssem.at[o],
            recv_sem=q_rsem.at[o],
            device_id=(kv_me, seq_peers[o]),
            device_id_type=MESH,
        )
        copy.start()
        q_copies.append(copy)
    own_q.wait()
    for copy in q_copies:
        copy.wait_recv()

    p_copies = []
    for j in range(kv_count):
        for s in range(slots):
            leaf = jnp.minimum(leaf_of[j * slots + s], leaves - 1)
            q_send[j, pl.ds(s * G, G), :] = q_all[leaf]
    own_page = pltpu.make_async_copy(q_send.at[kv_me], q_page.at[kv_me], own_sem.at[1])
    own_page.start()
    for o in range(1, kv_count):
        copy = pltpu.make_async_remote_copy(
            src_ref=q_send.at[kv_peers[o]],
            dst_ref=q_page.at[kv_me],
            send_sem=p_ssem.at[o],
            recv_sem=p_rsem.at[o],
            device_id=(kv_peers[o], seq_me),
            device_id_type=MESH,
        )
        copy.start()
        p_copies.append(copy)

    for copy in loads:
        copy.wait()

    def fold(op, value, init):
        for t in range(value.shape[1] // LANES):
            tile = value[:, t * LANES : (t + 1) * LANES]
            init = tile if init is None else op(init, tile)
        return init

    spans = [(at, min(CHUNK, prompt_rows - at), False) for at in range(0, prompt_rows, CHUNK)]
    spans += [
        (prompt_rows + at, min(CHUNK, branch_rows - at), True)
        for at in range(0, branch_rows, CHUNK)
    ]

    def shared_rows(i, _):
        first = pl.multiple_of(i * row_block, row_block)
        leaf_first = i * (row_block // G)
        q = q_all[pl.ds(leaf_first, row_block // G)].reshape(row_block, head_dim)
        peak = None
        for at, size, masked in spans:
            s = lax.dot_general(
                q, kbuf[pl.ds(at, size), :], NT, preferred_element_type=jnp.float32
            )
            if masked:
                place = lax.broadcasted_iota(jnp.int32, (1, size), 1) + (
                    seq_me * branch_rows + (at - prompt_rows)
                )
                own = row_branch[pl.ds(first, row_block), :][:, :1]
                s = jnp.where(own == place // BR_LEN, s, NEG)
            s_buf[:, pl.ds(at, size)] = s
            peak = fold(jnp.maximum, s, peak)
        top = jnp.max(peak, axis=1, keepdims=True)
        part, num = None, None
        for at, size, _masked in spans:
            expo = jnp.exp2((s_buf[:, pl.ds(at, size)] - top) * scale)
            part = fold(jnp.add, expo, part)
            step = jnp.dot(
                expo.astype(jnp.bfloat16),
                vbuf[pl.ds(at, size), :],
                preferred_element_type=jnp.float32,
            )
            num = step if num is None else num + step
        row_top[pl.ds(first, row_block), :] = jnp.broadcast_to(top, (row_block, LANES))
        row_sum[pl.ds(first, row_block), :] = jnp.broadcast_to(
            jnp.sum(part, axis=1, keepdims=True), (row_block, LANES)
        )
        row_num[pl.ds(first, row_block), :] = num
        return 0

    n_blocks = rows // row_block
    lax.fori_loop(0, n_blocks // 2, shared_rows, 0)

    own_page.wait()
    for copy in p_copies:
        copy.wait_recv()

    stat_lane = lax.broadcasted_iota(jnp.int32, (heads_all, col_w), 1)
    stat_row = lax.broadcasted_iota(jnp.int32, (heads_all, col_w), 0) % G
    token_col = lax.broadcasted_iota(jnp.int32, (1, page_rows), 1)
    for s in range(slots):
        page_loads[2 * s].wait()
        page_loads[2 * s + 1].wait()
        q = q_page[:, pl.ds(s * G, G), :].reshape(heads_all, head_dim)
        scores = lax.dot_general(q, pkbuf[s], NT, preferred_element_type=jnp.float32)
        limit = jnp.where(token_col < valid_of[s] * kv_count, 0.0, NEG)
        scores = scores + (head_bias[...] + limit)
        top = jnp.max(fold(jnp.maximum, scores, None), axis=1, keepdims=True)
        expo = jnp.exp2((scores - top) * scale)
        psum = jnp.sum(fold(jnp.add, expo, None), axis=1, keepdims=True)
        num = jnp.dot(expo.astype(jnp.bfloat16), pvbuf[s], preferred_element_type=jnp.float32)
        num_send[:, pl.ds(s * G, G), :] = num.astype(jnp.bfloat16).reshape(
            kv_count, G, head_dim
        )
        here = stat_lane == stat_row + s * G
        stat_top[...] = jnp.where(here, top, stat_top[...])
        stat_sum[...] = jnp.where(here, psum, stat_sum[...])
    for j in range(kv_count):
        span = pl.ds(j * G, G)
        stat_send[j, 0:1, :] = jnp.sum(stat_top[span, :], axis=0, keepdims=True)
        stat_send[j, 1:2, :] = jnp.sum(stat_sum[span, :], axis=0, keepdims=True)
    own_num = pltpu.make_async_copy(num_send.at[kv_me], num_recv.at[kv_me], own_sem.at[2])
    own_stat = pltpu.make_async_copy(stat_send.at[kv_me], stat_recv.at[kv_me], own_sem.at[3])
    own_num.start()
    own_stat.start()
    n_copies = []
    for o in range(1, kv_count):
        for which, (src, dst) in enumerate(((num_send, num_recv), (stat_send, stat_recv))):
            copy = pltpu.make_async_remote_copy(
                src_ref=src.at[kv_peers[o]],
                dst_ref=dst.at[kv_me],
                send_sem=n_ssem.at[which, o],
                recv_sem=n_rsem.at[which, o],
                device_id=(kv_peers[o], seq_me),
                device_id_type=MESH,
            )
            copy.start()
            n_copies.append(copy)

    lax.fori_loop(n_blocks // 2, n_blocks, shared_rows, 0)

    col = lax.broadcasted_iota(jnp.int32, (1, n_col), 1)
    target = jnp.full((1, n_col), rows, jnp.int32)
    for j in range(kv_count):
        for s in range(slots):
            at = j * col_w + s * G
            inside = (col >= at) & (col < at + G)
            target = jnp.where(inside, leaf_of[j * slots + s] * G + (col - at), target)

    own_num.wait()
    own_stat.wait()
    for copy in n_copies:
        copy.wait_recv()

    col_top = jnp.concatenate([stat_recv[j, 0:1, :] for j in range(kv_count)], axis=1)
    col_sum = jnp.concatenate([stat_recv[j, 1:2, :] for j in range(kv_count)], axis=1)
    col_num = num_recv[...].reshape(n_col, head_dim)
    own_row = lax.broadcasted_iota(jnp.int32, (own_rows, n_col), 0)
    diag = lax.broadcasted_iota(jnp.int32, (own_rows, LANES), 0) == lax.broadcasted_iota(
        jnp.int32, (own_rows, LANES), 1
    )

    def merged(dest):
        first = pl.multiple_of(dest * own_rows, own_rows)
        base = row_top[pl.ds(first, own_rows), :][:, :1]
        match = (own_row + first) == target
        seen = jnp.where(match, col_top, NEG)
        top = jnp.maximum(base, jnp.max(fold(jnp.maximum, seen, None), axis=1, keepdims=True))
        weight = jnp.where(match, jnp.exp2((seen - top) * scale), 0.0)
        factor = jnp.exp2((base - top) * scale)
        den = row_sum[pl.ds(first, own_rows), :][:, :1] * factor + jnp.sum(
            fold(jnp.add, weight * col_sum, None), axis=1, keepdims=True
        )
        num = row_num[pl.ds(first, own_rows), :] * factor + jnp.dot(
            weight.astype(jnp.bfloat16), col_num, preferred_element_type=jnp.float32
        )
        return top, den, num

    f_copies = []
    for o in range(seq_count - 1, 0, -1):
        top, den, num = merged(seq_peers[o])
        fin_num_send[o] = num.astype(jnp.bfloat16)
        fin_stat_send[o, 0:1, :] = jnp.sum(jnp.where(diag, top, 0.0), axis=0, keepdims=True)
        fin_stat_send[o, 1:2, :] = jnp.sum(jnp.where(diag, den, 0.0), axis=0, keepdims=True)
        for which, (src, dst) in enumerate(
            ((fin_stat_send, fin_stat_recv), (fin_num_send, fin_num_recv))
        ):
            copy = pltpu.make_async_remote_copy(
                src_ref=src.at[o],
                dst_ref=dst.at[o],
                send_sem=f_ssem.at[which, o],
                recv_sem=f_rsem.at[which, o],
                device_id=(kv_me, seq_peers[o]),
                device_id_type=MESH,
            )
            copy.start()
            f_copies.append(copy)
    top, den, num = merged(seq_me)

    for copy in f_copies:
        copy.wait_recv()
    tops, dens = [top], [den]
    for o in range(1, seq_count):
        tops.append(
            jnp.sum(jnp.where(diag, fin_stat_recv[o, 0:1, :], 0.0), axis=1, keepdims=True)
        )
        dens.append(
            jnp.sum(jnp.where(diag, fin_stat_recv[o, 1:2, :], 0.0), axis=1, keepdims=True)
        )
    best = functools.reduce(jnp.maximum, tops)
    scale_own = jnp.exp2((top - best) * scale)
    den, num = den * scale_own, num * scale_own
    for o in range(1, seq_count):
        factor = jnp.exp2((tops[o] - best) * scale)
        den = den + dens[o] * factor
        num = num + fin_num_recv[o].astype(jnp.float32) * factor
    out[...] = (num / den).astype(out.dtype).reshape(out.shape)

    for copy in q_copies + p_copies + n_copies + f_copies:
        copy.wait_send()


def body(
    queries,
    prompt_keys,
    prompt_values,
    branch_keys,
    branch_values,
    pool_keys,
    pool_values,
    suffix_lengths,
    leaf_branch,
    slot_item,
):
    kv_count = lax.axis_size("kv")
    seq_count = lax.axis_size("seq")
    leaf_dev, heads_dev, head_dim = queries.shape
    slots, block, kvh_all = pool_keys.shape[:3]
    assert heads_dev == G and kvh_all == kv_count and leaf_dev * G <= LANES
    rows = leaf_dev * seq_count * G
    own_rows = leaf_dev * G
    prompt_keys, prompt_values, branch_keys, branch_values = (
        x.reshape(x.shape[1:]) for x in (prompt_keys, prompt_values, branch_keys, branch_values)
    )
    pool_keys, pool_values = (
        x.reshape(slots, block * kvh_all, head_dim) for x in (pool_keys, pool_values)
    )
    keys = prompt_keys.shape[0] + branch_keys.shape[0]
    page_rows = block * kvh_all
    heads_all = kv_count * G
    col_w = -(-slots * G // LANES) * LANES
    row_block = min(256, rows // 2)
    f32, bf16, i32 = jnp.float32, jnp.bfloat16, jnp.int32
    any_spec = pl.BlockSpec(memory_space=pl.ANY)
    smem = pl.BlockSpec(memory_space=pltpu.SMEM)
    dma = pltpu.SemaphoreType.DMA
    return pl.pallas_call(
        functools.partial(kernel, kv_count, seq_count),
        out_shape=jax.ShapeDtypeStruct(queries.shape, queries.dtype),
        in_specs=[smem] * 3 + [any_spec] * 7,
        out_specs=pl.BlockSpec(memory_space=pltpu.VMEM),
        scratch_shapes=[
            pltpu.SMEM((leaf_dev * seq_count,), i32),
            pltpu.SMEM((kv_count * slots,), i32),
            pltpu.SMEM((slots,), i32),
            pltpu.VMEM((keys, head_dim), bf16),
            pltpu.VMEM((keys, head_dim), bf16),
            pltpu.VMEM((slots, page_rows, head_dim), bf16),
            pltpu.VMEM((slots, page_rows, head_dim), bf16),
            pltpu.VMEM((leaf_dev * seq_count, G, head_dim), bf16),
            pltpu.VMEM((kv_count, slots * G, head_dim), bf16),
            pltpu.VMEM((kv_count, slots * G, head_dim), bf16),
            pltpu.VMEM((rows, LANES), i32),
            pltpu.VMEM((heads_all, page_rows), f32),
            pltpu.VMEM((row_block, keys), f32),
            pltpu.VMEM((rows, LANES), f32),
            pltpu.VMEM((rows, LANES), f32),
            pltpu.VMEM((rows, head_dim), f32),
            pltpu.VMEM((heads_all, col_w), f32),
            pltpu.VMEM((heads_all, col_w), f32),
            pltpu.VMEM((kv_count, col_w, head_dim), bf16),
            pltpu.VMEM((kv_count, col_w, head_dim), bf16),
            pltpu.VMEM((kv_count, 8, col_w), f32),
            pltpu.VMEM((kv_count, 8, col_w), f32),
            pltpu.VMEM((seq_count, own_rows, head_dim), bf16),
            pltpu.VMEM((seq_count, own_rows, head_dim), bf16),
            pltpu.VMEM((seq_count, 8, LANES), f32),
            pltpu.VMEM((seq_count, 8, LANES), f32),
            dma((4,)),
            dma((2, slots)),
            dma((4,)),
            dma((seq_count,)),
            dma((seq_count,)),
            dma((kv_count,)),
            dma((kv_count,)),
            dma((2, kv_count)),
            dma((2, kv_count)),
            dma((2, seq_count)),
            dma((2, seq_count)),
        ],
        compiler_params=pltpu.CompilerParams(
            collective_id=0, has_side_effects=True, vmem_limit_bytes=60 * 1024 * 1024
        ),
        name="attend",
    )(
        suffix_lengths,
        leaf_branch,
        slot_item,
        queries,
        prompt_keys,
        prompt_values,
        branch_keys,
        branch_values,
        pool_keys,
        pool_values,
    )


def solution(mesh):
    return jax.shard_map(
        body,
        mesh=mesh,
        in_specs=(
            P("seq", "kv", None),
            P("kv", "seq", None),
            P("kv", "seq", None),
            P("kv", "seq", None),
            P("kv", "seq", None),
            P(("kv", "seq"), None, None, None),
            P(("kv", "seq"), None, None, None),
            P(),
            P(),
            P(),
        ),
        out_specs=P("seq", "kv", None),
        check_vma=False,
    )
```

```python
import functools
import math

import jax
import jax.numpy as jnp
from jax import lax
from jax.experimental import pallas as pl
from jax.experimental.pallas import tpu as pltpu
from jax.sharding import PartitionSpec as P

G = 16
BR_LEN = 4096
NEG = -1e30
LANES = 128
CHUNK = 1024
MESH = pl.DeviceIdType.MESH
NT = (((1,), (1,)), ((), ()))


def kernel(
    kv_count,
    seq_count,
    lengths_in,
    branch_in,
    items_in,
    queries,
    prompt_k,
    prompt_v,
    branch_k,
    branch_v,
    pool_k,
    pool_v,
    out,
    lengths,
    branch_of,
    items,
    ends,
    leaf_of,
    valid_of,
    kbuf,
    vbuf,
    pkbuf,
    pvbuf,
    q_all,
    q_send,
    q_page,
    row_branch,
    head_bias,
    s_buf,
    row_top,
    row_sum,
    row_num,
    stat_top,
    stat_sum,
    num_send,
    num_recv,
    stat_send,
    stat_recv,
    fin_num_send,
    fin_num_recv,
    fin_stat_send,
    fin_stat_recv,
    table_sem,
    load_sem,
    page_sem,
    own_sem,
    q_ssem,
    q_rsem,
    p_ssem,
    p_rsem,
    n_ssem,
    n_rsem,
    f_ssem,
    f_rsem,
):
    kv_me = lax.axis_index("kv")
    seq_me = lax.axis_index("seq")
    leaf_dev = queries.shape[0]
    head_dim = queries.shape[2]
    leaves = leaf_dev * seq_count
    rows = leaves * G
    own_rows = leaf_dev * G
    slots, page_rows = pool_k.shape[0], pool_k.shape[1]
    block = page_rows // kv_count
    prompt_rows, branch_rows = prompt_k.shape[0], branch_k.shape[0]
    keys = prompt_rows + branch_rows
    col_w = num_send.shape[1]
    n_col = kv_count * col_w
    heads_all = kv_count * G
    scale = math.log2(math.e) / math.sqrt(head_dim)
    row_block = min(256, rows // 2)

    loads = [
        pltpu.make_async_copy(prompt_k, kbuf.at[pl.ds(0, prompt_rows)], load_sem.at[0]),
        pltpu.make_async_copy(branch_k, kbuf.at[pl.ds(prompt_rows, branch_rows)], load_sem.at[1]),
        pltpu.make_async_copy(prompt_v, vbuf.at[pl.ds(0, prompt_rows)], load_sem.at[2]),
        pltpu.make_async_copy(branch_v, vbuf.at[pl.ds(prompt_rows, branch_rows)], load_sem.at[3]),
    ]
    page_loads = []
    for s in range(slots):
        page_loads.append(pltpu.make_async_copy(pool_k.at[s], pkbuf.at[s], page_sem.at[0, s]))
        page_loads.append(pltpu.make_async_copy(pool_v.at[s], pvbuf.at[s], page_sem.at[1, s]))
    own_q = pltpu.make_async_copy(
        queries, q_all.at[pl.ds(seq_me * leaf_dev, leaf_dev)], own_sem.at[0]
    )

    seq_peers = [lax.rem(seq_me + o, seq_count) for o in range(seq_count)]
    kv_peers = [lax.rem(kv_me + o, kv_count) for o in range(kv_count)]

    barrier = pltpu.get_barrier_semaphore()
    for o in range(1, kv_count):
        pl.semaphore_signal(barrier, inc=1, device_id=(kv_peers[o], seq_me), device_id_type=MESH)
    for o in range(1, seq_count):
        pl.semaphore_signal(barrier, inc=1, device_id=(kv_me, seq_peers[o]), device_id_type=MESH)
    tables = [
        pltpu.make_async_copy(lengths_in, lengths, table_sem.at[0]),
        pltpu.make_async_copy(branch_in, branch_of, table_sem.at[1]),
        pltpu.make_async_copy(items_in, items, table_sem.at[2]),
    ]
    for copy in tables:
        copy.start()
    own_q.start()
    for copy in loads:
        copy.start()
    for copy in page_loads:
        copy.start()

    for copy in tables:
        copy.wait()
    total = jnp.int32(0)
    for l in range(leaves):
        total = total + (lengths[l] + (block - 1)) // block
        ends[l] = total
    for j in range(kv_count):
        for s in range(slots):
            item = items[(j * seq_count + seq_me) * slots + s]

            def count(l, acc, item=item):
                return acc + (item >= ends[l]).astype(jnp.int32)

            leaf_of[j * slots + s] = lax.fori_loop(0, leaves, count, jnp.int32(0), unroll=True)
    for s in range(slots):
        item = items[(kv_me * seq_count + seq_me) * slots + s]
        leaf = leaf_of[kv_me * slots + s]
        safe = jnp.minimum(leaf, leaves - 1)
        length = lengths[safe]
        start = ends[safe] - (length + (block - 1)) // block
        live = jnp.clip(length - (item - start) * block, 0, block)
        valid_of[s] = jnp.where(leaf < leaves, live, 0)

    for l in range(leaves):
        row_branch[pl.ds(l * G, G), :] = jnp.full((G, LANES), branch_of[l], jnp.int32)
    bias_col = lax.broadcasted_iota(jnp.int32, (heads_all, page_rows), 1) % kv_count
    bias_row = lax.broadcasted_iota(jnp.int32, (heads_all, page_rows), 0) // G
    head_bias[...] = jnp.where(bias_col == bias_row, 0.0, NEG)
    stat_top[...] = jnp.zeros_like(stat_top)
    stat_sum[...] = jnp.zeros_like(stat_sum)
    if col_w > slots * G:
        num_send[...] = jnp.zeros_like(num_send)
        rest = col_w - slots * G
        num_recv[:, pl.ds(slots * G, rest), :] = jnp.zeros(
            (kv_count, rest, head_dim), num_recv.dtype
        )

    pl.semaphore_wait(barrier, kv_count + seq_count - 2)

    q_copies = []
    for o in range(seq_count - 1, 0, -1):
        copy = pltpu.make_async_remote_copy(
            src_ref=queries,
            dst_ref=q_all.at[pl.ds(seq_me * leaf_dev, leaf_dev)],
            send_sem=q_ssem.at[o],
            recv_sem=q_rsem.at[o],
            device_id=(kv_me, seq_peers[o]),
            device_id_type=MESH,
        )
        copy.start()
        q_copies.append(copy)
    own_q.wait()
    for copy in q_copies:
        copy.wait_recv()

    p_copies = []

    def pick(j):
        for s in range(slots):
            leaf = jnp.minimum(leaf_of[j * slots + s], leaves - 1)
            q_send[j, pl.ds(s * G, G), :] = q_all[leaf]

    for o in range(1, kv_count):
        pick(kv_peers[o])
        copy = pltpu.make_async_remote_copy(
            src_ref=q_send.at[kv_peers[o]],
            dst_ref=q_page.at[kv_me],
            send_sem=p_ssem.at[o],
            recv_sem=p_rsem.at[o],
            device_id=(kv_peers[o], seq_me),
            device_id_type=MESH,
        )
        copy.start()
        p_copies.append(copy)
    pick(kv_me)
    own_page = pltpu.make_async_copy(q_send.at[kv_me], q_page.at[kv_me], own_sem.at[1])
    own_page.start()

    for copy in loads:
        copy.wait()

    def fold(op, value, init):
        for t in range(value.shape[1] // LANES):
            tile = value[:, t * LANES : (t + 1) * LANES]
            init = tile if init is None else op(init, tile)
        return init

    spans = [(at, min(CHUNK, prompt_rows - at), False) for at in range(0, prompt_rows, CHUNK)]
    spans += [
        (prompt_rows + at, min(CHUNK, branch_rows - at), True)
        for at in range(0, branch_rows, CHUNK)
    ]

    def shared_rows(i, _):
        first = pl.multiple_of(i * row_block, row_block)
        leaf_first = i * (row_block // G)
        q = q_all[pl.ds(leaf_first, row_block // G)].reshape(row_block, head_dim)
        peak = None
        for at, size, masked in spans:
            s = lax.dot_general(
                q, kbuf[pl.ds(at, size), :], NT, preferred_element_type=jnp.float32
            )
            if masked:
                place = lax.broadcasted_iota(jnp.int32, (1, size), 1) + (
                    seq_me * branch_rows + (at - prompt_rows)
                )
                own = row_branch[pl.ds(first, row_block), :][:, :1]
                s = jnp.where(own == place // BR_LEN, s, NEG)
            s_buf[:, pl.ds(at, size)] = s
            peak = fold(jnp.maximum, s, peak)
        top = jnp.max(peak, axis=1, keepdims=True)
        part, num = None, None
        for at, size, _masked in spans:
            expo = jnp.exp2((s_buf[:, pl.ds(at, size)] - top) * scale)
            part = fold(jnp.add, expo, part)
            step = jnp.dot(
                expo.astype(jnp.bfloat16),
                vbuf[pl.ds(at, size), :],
                preferred_element_type=jnp.float32,
            )
            num = step if num is None else num + step
        row_top[pl.ds(first, row_block), :] = jnp.broadcast_to(top, (row_block, LANES))
        row_sum[pl.ds(first, row_block), :] = jnp.broadcast_to(
            jnp.sum(part, axis=1, keepdims=True), (row_block, LANES)
        )
        row_num[pl.ds(first, row_block), :] = num
        return 0

    n_blocks = rows // row_block
    lax.fori_loop(0, n_blocks // 2, shared_rows, 0)

    own_page.wait()
    for copy in p_copies:
        copy.wait_recv()

    stat_lane = lax.broadcasted_iota(jnp.int32, (heads_all, col_w), 1)
    stat_row = lax.broadcasted_iota(jnp.int32, (heads_all, col_w), 0) % G
    per = max(1, slots // 4)
    n_copies = []

    def give(src, dst, part, o):
        copy = pltpu.make_async_remote_copy(
            src_ref=src,
            dst_ref=dst,
            send_sem=n_ssem.at[part, o],
            recv_sem=n_rsem.at[part, o],
            device_id=(kv_peers[o], seq_me),
            device_id_type=MESH,
        )
        copy.start()
        n_copies.append(copy)

    token_col = lax.broadcasted_iota(jnp.int32, (1, page_rows), 1)
    for s in range(slots):
        page_loads[2 * s].wait()
        page_loads[2 * s + 1].wait()
        q = q_page[:, pl.ds(s * G, G), :].reshape(heads_all, head_dim)
        scores = lax.dot_general(q, pkbuf[s], NT, preferred_element_type=jnp.float32)
        limit = jnp.where(token_col < valid_of[s] * kv_count, 0.0, NEG)
        scores = scores + (head_bias[...] + limit)
        top = jnp.max(fold(jnp.maximum, scores, None), axis=1, keepdims=True)
        expo = jnp.exp2((scores - top) * scale)
        psum = jnp.sum(fold(jnp.add, expo, None), axis=1, keepdims=True)
        num = jnp.dot(expo.astype(jnp.bfloat16), pvbuf[s], preferred_element_type=jnp.float32)
        num_send[:, pl.ds(s * G, G), :] = num.astype(jnp.bfloat16).reshape(
            kv_count, G, head_dim
        )
        here = stat_lane == stat_row + s * G
        stat_top[...] = jnp.where(here, top, stat_top[...])
        stat_sum[...] = jnp.where(here, psum, stat_sum[...])
        if s % per == per - 1:
            span = pl.ds((s + 1 - per) * G, per * G)
            for o in range(1, kv_count):
                give(num_send.at[kv_peers[o], span], num_recv.at[kv_me, span], s // per, o)
    for j in range(kv_count):
        span = pl.ds(j * G, G)
        stat_send[j, 0:1, :] = jnp.sum(stat_top[span, :], axis=0, keepdims=True)
        stat_send[j, 1:2, :] = jnp.sum(stat_sum[span, :], axis=0, keepdims=True)
    own_num = pltpu.make_async_copy(
        num_send.at[kv_me, pl.ds(0, slots * G)],
        num_recv.at[kv_me, pl.ds(0, slots * G)],
        own_sem.at[2],
    )
    own_stat = pltpu.make_async_copy(stat_send.at[kv_me], stat_recv.at[kv_me], own_sem.at[3])
    own_num.start()
    own_stat.start()
    for o in range(1, kv_count):
        give(stat_send.at[kv_peers[o]], stat_recv.at[kv_me], slots // per, o)

    lax.fori_loop(n_blocks // 2, n_blocks, shared_rows, 0)

    col = lax.broadcasted_iota(jnp.int32, (1, n_col), 1)
    target = jnp.full((1, n_col), rows, jnp.int32)
    for j in range(kv_count):
        for s in range(slots):
            at = j * col_w + s * G
            inside = (col >= at) & (col < at + G)
            target = jnp.where(inside, leaf_of[j * slots + s] * G + (col - at), target)

    own_num.wait()
    own_stat.wait()
    for copy in n_copies:
        copy.wait_recv()

    col_top = jnp.concatenate([stat_recv[j, 0:1, :] for j in range(kv_count)], axis=1)
    col_sum = jnp.concatenate([stat_recv[j, 1:2, :] for j in range(kv_count)], axis=1)
    col_num = num_recv[...].reshape(n_col, head_dim)
    own_row = lax.broadcasted_iota(jnp.int32, (own_rows, n_col), 0)
    diag = lax.broadcasted_iota(jnp.int32, (own_rows, LANES), 0) == lax.broadcasted_iota(
        jnp.int32, (own_rows, LANES), 1
    )

    def merged(dest):
        first = pl.multiple_of(dest * own_rows, own_rows)
        base = row_top[pl.ds(first, own_rows), :][:, :1]
        match = (own_row + first) == target
        seen = jnp.where(match, col_top, NEG)
        top = jnp.maximum(base, jnp.max(fold(jnp.maximum, seen, None), axis=1, keepdims=True))
        weight = jnp.where(match, jnp.exp2((seen - top) * scale), 0.0)
        factor = jnp.exp2((base - top) * scale)
        den = row_sum[pl.ds(first, own_rows), :][:, :1] * factor + jnp.sum(
            fold(jnp.add, weight * col_sum, None), axis=1, keepdims=True
        )
        num = row_num[pl.ds(first, own_rows), :] * factor + jnp.dot(
            weight.astype(jnp.bfloat16), col_num, preferred_element_type=jnp.float32
        )
        return top, den, num

    f_copies = []
    for o in range(seq_count - 1, 0, -1):
        top, den, num = merged(seq_peers[o])
        fin_num_send[o] = num.astype(jnp.bfloat16)
        fin_stat_send[o, 0:1, :] = jnp.sum(jnp.where(diag, top, 0.0), axis=0, keepdims=True)
        fin_stat_send[o, 1:2, :] = jnp.sum(jnp.where(diag, den, 0.0), axis=0, keepdims=True)
        for which, (src, dst) in enumerate(
            ((fin_stat_send, fin_stat_recv), (fin_num_send, fin_num_recv))
        ):
            copy = pltpu.make_async_remote_copy(
                src_ref=src.at[o],
                dst_ref=dst.at[o],
                send_sem=f_ssem.at[which, o],
                recv_sem=f_rsem.at[which, o],
                device_id=(kv_me, seq_peers[o]),
                device_id_type=MESH,
            )
            copy.start()
            f_copies.append(copy)
    top, den, num = merged(seq_me)

    for copy in f_copies:
        copy.wait_recv()
    tops, dens = [top], [den]
    for o in range(1, seq_count):
        tops.append(
            jnp.sum(jnp.where(diag, fin_stat_recv[o, 0:1, :], 0.0), axis=1, keepdims=True)
        )
        dens.append(
            jnp.sum(jnp.where(diag, fin_stat_recv[o, 1:2, :], 0.0), axis=1, keepdims=True)
        )
    best = functools.reduce(jnp.maximum, tops)
    scale_own = jnp.exp2((top - best) * scale)
    den, num = den * scale_own, num * scale_own
    for o in range(1, seq_count):
        factor = jnp.exp2((tops[o] - best) * scale)
        den = den + dens[o] * factor
        num = num + fin_num_recv[o].astype(jnp.float32) * factor
    out[...] = (num / den).astype(out.dtype).reshape(out.shape)

    for copy in q_copies + p_copies + n_copies + f_copies:
        copy.wait_send()


def body(
    queries,
    prompt_keys,
    prompt_values,
    branch_keys,
    branch_values,
    pool_keys,
    pool_values,
    suffix_lengths,
    leaf_branch,
    slot_item,
):
    kv_count = lax.axis_size("kv")
    seq_count = lax.axis_size("seq")
    leaf_dev, heads_dev, head_dim = queries.shape
    slots, block, kvh_all = pool_keys.shape[:3]
    assert heads_dev == G and kvh_all == kv_count and leaf_dev * G <= LANES
    rows = leaf_dev * seq_count * G
    own_rows = leaf_dev * G
    prompt_keys, prompt_values, branch_keys, branch_values = (
        x.reshape(x.shape[1:]) for x in (prompt_keys, prompt_values, branch_keys, branch_values)
    )
    pool_keys, pool_values = (
        x.reshape(slots, block * kvh_all, head_dim) for x in (pool_keys, pool_values)
    )
    keys = prompt_keys.shape[0] + branch_keys.shape[0]
    page_rows = block * kvh_all
    heads_all = kv_count * G
    col_w = -(-slots * G // LANES) * LANES
    row_block = min(256, rows // 2)
    f32, bf16, i32 = jnp.float32, jnp.bfloat16, jnp.int32
    any_spec = pl.BlockSpec(memory_space=pl.ANY)
    dma = pltpu.SemaphoreType.DMA
    return pl.pallas_call(
        functools.partial(kernel, kv_count, seq_count),
        out_shape=jax.ShapeDtypeStruct(queries.shape, queries.dtype),
        in_specs=[any_spec] * 10,
        out_specs=pl.BlockSpec(memory_space=pltpu.VMEM),
        scratch_shapes=[
            pltpu.SMEM(suffix_lengths.shape, i32),
            pltpu.SMEM(leaf_branch.shape, i32),
            pltpu.SMEM(slot_item.shape, i32),
            pltpu.SMEM((leaf_dev * seq_count,), i32),
            pltpu.SMEM((kv_count * slots,), i32),
            pltpu.SMEM((slots,), i32),
            pltpu.VMEM((keys, head_dim), bf16),
            pltpu.VMEM((keys, head_dim), bf16),
            pltpu.VMEM((slots, page_rows, head_dim), bf16),
            pltpu.VMEM((slots, page_rows, head_dim), bf16),
            pltpu.VMEM((leaf_dev * seq_count, G, head_dim), bf16),
            pltpu.VMEM((kv_count, slots * G, head_dim), bf16),
            pltpu.VMEM((kv_count, slots * G, head_dim), bf16),
            pltpu.VMEM((rows, LANES), i32),
            pltpu.VMEM((heads_all, page_rows), f32),
            pltpu.VMEM((row_block, keys), f32),
            pltpu.VMEM((rows, LANES), f32),
            pltpu.VMEM((rows, LANES), f32),
            pltpu.VMEM((rows, head_dim), f32),
            pltpu.VMEM((heads_all, col_w), f32),
            pltpu.VMEM((heads_all, col_w), f32),
            pltpu.VMEM((kv_count, col_w, head_dim), bf16),
            pltpu.VMEM((kv_count, col_w, head_dim), bf16),
            pltpu.VMEM((kv_count, 2, col_w), f32),
            pltpu.VMEM((kv_count, 2, col_w), f32),
            pltpu.VMEM((seq_count, own_rows, head_dim), bf16),
            pltpu.VMEM((seq_count, own_rows, head_dim), bf16),
            pltpu.VMEM((seq_count, 2, LANES), f32),
            pltpu.VMEM((seq_count, 2, LANES), f32),
            dma((3,)),
            dma((4,)),
            dma((2, slots)),
            dma((4,)),
            dma((seq_count,)),
            dma((seq_count,)),
            dma((kv_count,)),
            dma((kv_count,)),
            dma((slots // max(1, slots // 4) + 1, kv_count)),
            dma((slots // max(1, slots // 4) + 1, kv_count)),
            dma((2, seq_count)),
            dma((2, seq_count)),
        ],
        compiler_params=pltpu.CompilerParams(
            collective_id=0, has_side_effects=True, vmem_limit_bytes=60 * 1024 * 1024
        ),
        name="attend",
    )(
        suffix_lengths,
        leaf_branch,
        slot_item,
        queries,
        prompt_keys,
        prompt_values,
        branch_keys,
        branch_values,
        pool_keys,
        pool_values,
    )


def solution(mesh):
    return jax.shard_map(
        body,
        mesh=mesh,
        in_specs=(
            P("seq", "kv", None),
            P("kv", "seq", None),
            P("kv", "seq", None),
            P("kv", "seq", None),
            P("kv", "seq", None),
            P(("kv", "seq"), None, None, None),
            P(("kv", "seq"), None, None, None),
            P(),
            P(),
            P(),
        ),
        out_specs=P("seq", "kv", None),
        check_vma=False,
    )
```
